32 devices in a mesh: gx: 4 (over y, core), gy: 8 (over z, x).
Axes of the slice: x: 2, y: 2, z: 4, core: 2. Of those that a mesh axis runs over, the one named last changes fastest.
Arguments:
- a_tiles: bfloat16 [4, 8, 16, 27, 128, 128], P('gx', 'gy'), may hold values from -0.5 to 0.5
- p_tiles: bfloat16 [4, 8, 16, 128, 128], P('gx', 'gy'), may hold values from -1.5 to 1.5
- neighbours: int32 [4, 8, 16, 27], P('gx', 'gy'), may hold values from 0 to 143, as said below
- groups: int32 [4, 8, 16, 27], P('gx', 'gy'), may hold values from 0 to 7
- slots: int32 [4, 8, 16, 8], P('gx', 'gy'), may hold values from 0 to 26
- aggregates: int32 [4, 8, 16], P('gx', 'gy'), may hold values from 0 to 31, as said below
Outputs:
- coarse_tiles: float32 [4, 8, 4, 27, 128, 128], P('gx', 'gy')
The draws below stay inside these ranges and needn't reach their ends.
Inputs may be any that keep to these rules, and one draw needn't show every extreme that they name: `neighbours`: tile k of a fine row on device (x, y) names row q % 16 of device (x + q // 48 - 1, y + (q // 16) % 3 - 1), which is always on the mesh; tile 0 names the row itself. The owner of aggregate g is gy index g // 4, as its coarse row g % 4. At most 4 fine rows of one device have aggregates with one owner; in every slab one owner gets exactly 4 from every device of the slab.
All inputs are finite; a program needn't handle non-finite values.
Results may differ from the reference program's by a relative error of at most 0.005.
Values may be sent and summed in bfloat16 or wider, within the bound.
A program may use at most 128 MiB of HBM per device.

```python
import jax
import jax.numpy as jnp
from jax import lax

TILE = 128
K = 27
KF = 8
KC = 27
ROWS = 16
RC = 4
SLABS = 4
COLS = 8


def draw_neighbours(key, part):
    key_x, key_y, key_q = jax.random.split(jax.random.fold_in(key, 11), 3)
    shape = (SLABS, COLS, ROWS, K)
    pick_x = jax.random.randint(key_x, shape, 0, 4)
    pick_y = jax.random.randint(key_y, shape, 0, 4)
    step_x = pick_x - 1 - (pick_x >= 2).astype(jnp.int32)
    step_y = pick_y - 1 - (pick_y >= 2).astype(jnp.int32)
    slab_pos = jnp.arange(SLABS, dtype=jnp.int32)[:, None, None, None]
    col_pos = jnp.arange(COLS, dtype=jnp.int32)[None, :, None, None]
    step_x = jnp.where((slab_pos + step_x < 0) | (slab_pos + step_x >= SLABS), -step_x, step_x)
    step_y = jnp.where((col_pos + step_y < 0) | (col_pos + step_y >= COLS), -step_y, step_y)
    other = jax.random.randint(key_q, shape, 0, ROWS)
    is_diag = jnp.arange(K, dtype=jnp.int32)[None, None, None, :] == 0
    row_pos = jnp.broadcast_to(jnp.arange(ROWS, dtype=jnp.int32)[None, None, :, None], shape)
    step_x = jnp.where(is_diag, 0, step_x)
    step_y = jnp.where(is_diag, 0, step_y)
    other = jnp.where(is_diag, row_pos, other)
    return (((step_x + 1) * 3 + step_y + 1) * ROWS + other).astype(jnp.int32)


def draw_aggregates(key, part):
    row_cap = (2 * ROWS + COLS - 1) // COLS
    key_hot, key_dev = jax.random.split(jax.random.fold_in(key, 23), 2)
    hot = jax.random.randint(key_hot, (SLABS,), 0, COLS)

    def one_device(device_key, hot_one):
        key_a, key_b, key_c = jax.random.split(device_key, 3)
        spread = jax.random.permutation(key_a, (COLS - 1) * row_cap)[:ROWS - row_cap]
        others = spread // row_cap
        others = others + (others >= hot_one).astype(jnp.int32)
        owners = jnp.concatenate([jnp.full((row_cap,), hot_one, jnp.int32), others.astype(jnp.int32)])
        order = jax.random.permutation(key_b, ROWS)
        owners = owners[order]
        local_rows = jax.random.randint(key_c, (ROWS,), 0, RC)
        return (owners * RC + local_rows).astype(jnp.int32)
    device_keys = jax.random.split(key_dev, SLABS * COLS)
    hots = jnp.repeat(hot, COLS)
    result = jax.vmap(one_device)(device_keys, hots)
    return result.reshape(SLABS, COLS, ROWS)


def touch_ends(array, key, smallest, high):
    extent = array.shape
    place = [jax.random.randint(jax.random.fold_in(key, axis), (), 0, extent[axis]) for axis in range(len(extent))]
    array = array.at[tuple(place)].set(smallest)
    longest = extent.index(max(extent))
    place[longest] = (place[longest] + 1) % extent[longest]
    return array.at[tuple(place)].set(high)


def level_of(rng, dims, cuts, smallest, top_value):
    gain, own = 1.0, jax.random.fold_in(rng, 6)
    for position, blocks in cuts:
        draws = jnp.exp(jax.random.uniform(jax.random.fold_in(own, position), (blocks,), jnp.float32, smallest / len(cuts), top_value / len(cuts)))
        gain = gain * jnp.repeat(draws, dims[position] // blocks).reshape([-1 if axis == position else 1 for axis in range(len(dims))])
    return gain


def noise(stream_key, dims, width, reach, cuts=(), kind=jnp.bfloat16):
    values = width * jax.random.normal(stream_key, dims, jnp.float32)
    if cuts:
        values = values * level_of(stream_key, dims, cuts, -0.22, 0.18)
    return jnp.clip(values, -reach, reach).astype(kind)


def setup_inputs(seed: int = 0) -> dict:
    keys = jax.random.split(jax.random.key(seed), 7)
    return {
        "a_tiles": noise(keys[0], (SLABS, COLS, ROWS, K, TILE, TILE), TILE ** -0.5, 0.5, ((0, 4), (1, 8))),
        "p_tiles": noise(keys[1], (SLABS, COLS, ROWS, TILE, TILE), (TILE // 8) ** -0.5, 1.5, ((0, 4), (1, 8))),
        "neighbours": draw_neighbours(jax.random.fold_in(keys[6], 71), 0),
        "groups": touch_ends(jax.random.randint(keys[3], (SLABS, COLS, ROWS, K), 0, KF), jax.random.fold_in(keys[3], 1), 0, KF - 1).astype(jnp.int32),
        "slots": touch_ends(jax.random.randint(keys[4], (SLABS, COLS, ROWS, KF), 0, KC), jax.random.fold_in(keys[4], 1), 0, KC - 1).astype(jnp.int32),
        "aggregates": draw_aggregates(jax.random.fold_in(keys[6], 71), 0),
    }


def row_part(block, a_row, column_row, group_row, p_row):
    far_tiles = jnp.take(block, column_row, axis=0).astype(jnp.float32)
    products = jnp.einsum("kab,kbc->kac", a_row.astype(jnp.float32), far_tiles)
    picker = (group_row[:, None] == jnp.arange(KF, dtype=jnp.int32)[None, :]).astype(jnp.float32)
    summed = jnp.einsum("kf,kac->fac", picker, products).astype(jnp.bfloat16)
    contrib = jnp.einsum("ba,fbc->fac", p_row.astype(jnp.float32), summed.astype(jnp.float32))
    return contrib.astype(jnp.bfloat16)


def reference(a_tiles, p_tiles, neighbours, groups, slots, aggregates):
    padded = jnp.pad(p_tiles, ((1, 1), (1, 1), (0, 0), (0, 0), (0, 0)))
    slab_ids = jnp.repeat(jnp.arange(SLABS, dtype=jnp.int32), COLS)
    column_ids = jnp.tile(jnp.arange(COLS, dtype=jnp.int32), SLABS)
    zero = jnp.zeros((), jnp.int32)

    def device_part(inputs):
        slab_index, column_index, a_dev, col_dev, grp_dev, p_dev = inputs
        block = lax.dynamic_slice(padded, (slab_index.astype(jnp.int32), column_index.astype(jnp.int32), zero, zero, zero), (3, 3, ROWS, TILE, TILE))
        block = block.reshape(9 * ROWS, TILE, TILE)
        return lax.map(lambda items: row_part(block, items[0], items[1], items[2], items[3]), (a_dev, col_dev, grp_dev, p_dev))

    contrib = lax.map(device_part, (slab_ids, column_ids,
                                    a_tiles.reshape(SLABS * COLS, ROWS, K, TILE, TILE),
                                    neighbours.reshape(SLABS * COLS, ROWS, K),
                                    groups.reshape(SLABS * COLS, ROWS, K),
                                    p_tiles.reshape(SLABS * COLS, ROWS, TILE, TILE)))
    contrib = contrib.reshape(SLABS, COLS * ROWS * KF, TILE, TILE)

    def slab_part(inputs):
        slab_contrib, slab_aggs, slab_slots = inputs
        segment_ids = (slab_aggs[:, :, None] * KC + slab_slots).reshape(-1)
        return jax.ops.segment_sum(slab_contrib.astype(jnp.float32), segment_ids, num_segments=COLS * RC * KC)

    coarse = lax.map(slab_part, (contrib, aggregates, slots))
    return coarse.reshape(SLABS, COLS, RC, KC, TILE, TILE)
```

```python
import functools

import jax
import jax.numpy as jnp
from jax import lax
from jax.experimental import pallas as pl
from jax.experimental.pallas import tpu as pltpu
from jax.sharding import PartitionSpec as P

KC = 27
AGG = 4
CHUNKS = 1


def shifted(block, axis, step):
    count = lax.axis_size(axis)
    pairs = [(i, i + step) for i in range(count) if 0 <= i + step < count]
    return lax.ppermute(block, axis, pairs)


def halo(block):
    below, above = shifted(block, "gy", 1), shifted(block, "gy", -1)
    line = (below, block, above)
    low = [shifted(piece, "gx", 1) for piece in line]
    high = [shifted(piece, "gx", -1) for piece in line]
    return (*low, *line, *high)


def row_kernel(order, place, count, near, group, a_ref, *rest):
    pieces, (out_ref, table, sums, sems) = rest[:9], rest[9:]
    step = pl.program_id(0)
    tiles, rows = a_ref.shape[1], pieces[0].shape[0]
    touched = sums.shape[0]

    @pl.when(step == 0)
    def _():
        copies = [
            pltpu.make_async_copy(piece, table.at[pl.ds(j * rows, rows)], sems.at[j])
            for j, piece in enumerate(pieces)
        ]
        for copy in copies:
            copy.start()
        for copy in copies:
            copy.wait()

    @pl.when(step < count[0])
    def _():
        row = order[step]
        sums[...] = jnp.zeros_like(sums)
        for k in range(tiles):
            product = jnp.dot(
                a_ref[0, k], table[near[row, k]], preferred_element_type=jnp.float32
            )
            sums[group[row, k]] += product
        own = table[4 * rows + row]
        for f in range(touched):
            out_ref[0, f] = lax.dot_general(
                own,
                sums[f].astype(jnp.bfloat16),
                (((0,), (0,)), ((), ())),
                preferred_element_type=jnp.float32,
            ).astype(jnp.bfloat16)


def row_products(a_local, pieces, near, group, order, place, count, slot_total, touched):
    rows, tiles, size, _ = a_local.shape
    steps = order.shape[0]
    flops = 2 * steps * (tiles + touched) * size**3
    return pl.pallas_call(
        row_kernel,
        out_shape=jax.ShapeDtypeStruct((slot_total, touched, size, size), jnp.bfloat16),
        grid_spec=pltpu.PrefetchScalarGridSpec(
            num_scalar_prefetch=5,
            grid=(steps,),
            in_specs=[
                pl.BlockSpec(
                    (1, tiles, size, size), lambda i, order, *_: (order[i], 0, 0, 0)
                )
            ]
            + [pl.BlockSpec(memory_space=pl.ANY)] * 9,
            out_specs=pl.BlockSpec(
                (1, touched, size, size), lambda i, order, place, *_: (place[i], 0, 0, 0)
            ),
            scratch_shapes=[
                pltpu.VMEM((9 * rows, size, size), jnp.bfloat16),
                pltpu.VMEM((touched, size, size), jnp.float32),
                pltpu.SemaphoreType.DMA((9,)),
            ],
        ),
        compiler_params=pltpu.CompilerParams(vmem_limit_bytes=24 << 20),
        cost_estimate=pl.CostEstimate(
            flops=flops, bytes_accessed=2 * steps * (tiles + touched) * size**2, transcendentals=0
        ),
    )(order, place, count, near, group, a_local, *pieces)


def sum_kernel(carried, segment, valid, recv_ref, *rest):
    out_ref = rest[-1]
    step = pl.program_id(0)

    @pl.when(step == 0)
    def _():
        out_ref[...] = rest[0][...] if carried else jnp.zeros_like(out_ref)

    @pl.when(valid[step] > 0)
    def _():
        for f in range(recv_ref.shape[1]):
            out_ref[segment[step, f]] += recv_ref[0, f].astype(jnp.float32)


def coarse_sums(recv, segment, valid, total, previous):
    slot_total, touched, size, _ = recv.shape
    whole = pl.BlockSpec((total, size, size), lambda i, *_: (0, 0, 0), pipeline_mode=pl.Buffered(1))
    carried = previous is not None
    return pl.pallas_call(
        functools.partial(sum_kernel, carried),
        out_shape=jax.ShapeDtypeStruct((total, size, size), jnp.float32),
        grid_spec=pltpu.PrefetchScalarGridSpec(
            num_scalar_prefetch=2,
            grid=(slot_total,),
            in_specs=[pl.BlockSpec((1, touched, size, size), lambda i, *_: (i, 0, 0, 0))]
            + [whole] * carried,
            out_specs=pl.BlockSpec((total, size, size), lambda i, *_: (0, 0, 0)),
        ),
        compiler_params=pltpu.CompilerParams(vmem_limit_bytes=32 << 20),
        cost_estimate=pl.CostEstimate(
            flops=slot_total * touched * size**2,
            bytes_accessed=(2 * slot_total * touched + 4 * total) * size**2,
            transcendentals=0,
        ),
    )(segment, valid, recv, *([previous] if carried else []))


def shards(a_tiles, p_tiles, neighbours, groups, slots, aggregates):
    row_count = a_tiles.shape[2]
    touched = slots.shape[-1]
    size = a_tiles.shape[-1]
    owner_count = lax.axis_size("gy")
    row_cap = (2 * row_count + owner_count - 1) // owner_count
    coarse_rows = row_count // AGG
    total = coarse_rows * KC
    a_local, p_local = a_tiles[0, 0], p_tiles[0, 0]
    near, group = neighbours[0, 0], groups[0, 0]
    slot_local, aggregate = slots[0, 0], aggregates[0, 0]

    owners = aggregate // coarse_rows
    local_row = aggregate % coarse_rows
    indices = jnp.arange(row_count, dtype=jnp.int32)
    same_owner = owners[:, None] == owners[None, :]
    earlier = indices[:, None] > indices[None, :]
    rank = jnp.sum((same_owner & earlier).astype(jnp.int32), axis=1)
    chunks = min(CHUNKS, row_cap)
    width = row_cap // chunks
    position = (rank // width * owner_count + owners) * width + rank % width
    slot_total = owner_count * row_cap
    selector = jnp.arange(slot_total, dtype=jnp.int32)[:, None] == position[None, :]
    segments = local_row[:, None] * KC + slot_local
    meta = jnp.concatenate([jnp.ones_like(local_row)[:, None], segments], axis=1)
    meta_sent = jnp.sum(jnp.where(selector[:, :, None], meta[None], 0), axis=1)
    meta_sent = meta_sent.reshape(chunks, owner_count, width, touched + 1)
    meta_recv = lax.all_to_all(meta_sent, "gy", split_axis=1, concat_axis=1, tiled=True)
    meta_recv = meta_recv.reshape(chunks, owner_count * width, touched + 1)

    pieces = halo(p_local)
    coarse = None
    sent = []
    for chunk in range(chunks):
        steps = min(row_count, owner_count * width, row_count)
        active = rank // width == chunk
        count = jnp.sum(active.astype(jnp.int32))
        ahead = jnp.sum((active[None, :] & earlier).astype(jnp.int32), axis=1)
        wanted = jnp.minimum(jnp.arange(steps, dtype=jnp.int32), count - 1)
        chosen = active[None, :] & (ahead[None, :] == wanted[:, None])
        order = jnp.sum(jnp.where(chosen, indices[None, :], 0), axis=1)
        place = jnp.sum(jnp.where(chosen, (owners * width + rank % width)[None, :], 0), axis=1)
        sent.append(
            row_products(
                a_local, pieces, near, group, order, place, count[None],
                owner_count * width, touched,
            )
        )
    recv = [lax.all_to_all(s, "gy", split_axis=0, concat_axis=0, tiled=True) for s in sent]
    for chunk in range(chunks):
        coarse = coarse_sums(
            recv[chunk], meta_recv[chunk, :, 1:], meta_recv[chunk, :, 0], total, coarse
        )
    return coarse.reshape(1, 1, coarse_rows, KC, size, size)


def solution(mesh):
    return jax.shard_map(
        shards,
        mesh=mesh,
        in_specs=(
            P("gx", "gy", None, None, None, None),
            P("gx", "gy", None, None, None),
            P("gx", "gy", None, None),
            P("gx", "gy", None, None),
            P("gx", "gy", None, None),
            P("gx", "gy", None),
        ),
        out_specs=P("gx", "gy", None, None, None, None),
        check_vma=False,
    )
```

```python
import functools
import math

import jax
import jax.numpy as jnp
from jax import lax
from jax.experimental import pallas as pl
from jax.experimental.pallas import tpu as pltpu
from jax.sharding import PartitionSpec as P

KC = 27
AGG = 4
CHUNKS = 1


def shifted(block, axis, step):
    count = lax.axis_size(axis)
    pairs = [(i, i + step) for i in range(count) if 0 <= i + step < count]
    return lax.ppermute(block, axis, pairs)


def halo(block):
    below, above = shifted(block, "gy", 1), shifted(block, "gy", -1)
    line = (below, block, above)
    low = [shifted(piece, "gx", 1) for piece in line]
    high = [shifted(piece, "gx", -1) for piece in line]
    return (*low, *line, *high)


def row_kernel(order, place, count, near, group, a_ref, *rest):
    pieces, (out_ref, table, sums, sems) = rest[:9], rest[9:]
    step = pl.program_id(0)
    tiles, rows = a_ref.shape[1], pieces[0].shape[0]
    touched = sums.shape[0]

    @pl.when(step == 0)
    def _():
        copies = [
            pltpu.make_async_copy(piece, table.at[pl.ds(j * rows, rows)], sems.at[j])
            for j, piece in enumerate(pieces)
        ]
        for copy in copies:
            copy.start()
        for copy in copies:
            copy.wait()

    @pl.when(step < count[0])
    def _():
        row = order[step]
        sums[...] = jnp.zeros_like(sums)
        for k in range(tiles):
            product = jnp.dot(
                a_ref[0, k], table[near[row, k]], preferred_element_type=jnp.float32
            )
            sums[group[row, k]] += product
        own = table[4 * rows + row]
        for f in range(touched):
            out_ref[0, f] = lax.dot_general(
                own,
                sums[f].astype(jnp.bfloat16),
                (((0,), (0,)), ((), ())),
                preferred_element_type=jnp.float32,
            ).astype(jnp.bfloat16)


def row_products(a_local, pieces, near, group, order, place, count, slot_total, touched):
    rows, tiles, size, _ = a_local.shape
    steps = order.shape[0]
    flops = 2 * steps * (tiles + touched) * size**3
    return pl.pallas_call(
        row_kernel,
        out_shape=jax.ShapeDtypeStruct((slot_total, touched, size, size), jnp.bfloat16),
        grid_spec=pltpu.PrefetchScalarGridSpec(
            num_scalar_prefetch=5,
            grid=(steps,),
            in_specs=[
                pl.BlockSpec(
                    (1, tiles, size, size), lambda i, order, *_: (order[i], 0, 0, 0)
                )
            ]
            + [pl.BlockSpec(memory_space=pl.ANY)] * 9,
            out_specs=pl.BlockSpec(
                (1, touched, size, size), lambda i, order, place, *_: (place[i], 0, 0, 0)
            ),
            scratch_shapes=[
                pltpu.VMEM((9 * rows, size, size), jnp.bfloat16),
                pltpu.VMEM((touched, size, size), jnp.float32),
                pltpu.SemaphoreType.DMA((9,)),
            ],
        ),
        compiler_params=pltpu.CompilerParams(vmem_limit_bytes=60 << 20),
        cost_estimate=pl.CostEstimate(
            flops=flops, bytes_accessed=2 * steps * (tiles + touched) * size**2, transcendentals=0
        ),
    )(order, place, count, near, group, a_local, *pieces)


def sum_kernel(carried, segment, valid, recv_ref, *rest):
    out_ref = rest[-1]
    step = pl.program_id(0)

    @pl.when(step == 0)
    def _():
        out_ref[...] = rest[0][...] if carried else jnp.zeros_like(out_ref)

    batch = recv_ref.shape[0]
    for j in range(batch):
        slot = step * batch + j

        @pl.when(valid[slot] > 0)
        def _():
            for f in range(recv_ref.shape[1]):
                out_ref[segment[slot, f]] += recv_ref[j, f].astype(jnp.float32)


def coarse_sums(recv, segment, valid, total, previous):
    slot_total, touched, size, _ = recv.shape
    whole = pl.BlockSpec((total, size, size), lambda i, *_: (0, 0, 0), pipeline_mode=pl.Buffered(1))
    carried = previous is not None
    batch = math.gcd(slot_total, 4)
    return pl.pallas_call(
        functools.partial(sum_kernel, carried),
        out_shape=jax.ShapeDtypeStruct((total, size, size), jnp.float32),
        grid_spec=pltpu.PrefetchScalarGridSpec(
            num_scalar_prefetch=2,
            grid=(slot_total // batch,),
            in_specs=[pl.BlockSpec((batch, touched, size, size), lambda i, *_: (i, 0, 0, 0))]
            + [whole] * carried,
            out_specs=pl.BlockSpec((total, size, size), lambda i, *_: (0, 0, 0)),
        ),
        compiler_params=pltpu.CompilerParams(vmem_limit_bytes=60 << 20),
        cost_estimate=pl.CostEstimate(
            flops=slot_total * touched * size**2,
            bytes_accessed=(2 * slot_total * touched + 4 * total) * size**2,
            transcendentals=0,
        ),
    )(segment, valid, recv, *([previous] if carried else []))


def shards(a_tiles, p_tiles, neighbours, groups, slots, aggregates):
    row_count = a_tiles.shape[2]
    touched = slots.shape[-1]
    size = a_tiles.shape[-1]
    owner_count = lax.axis_size("gy")
    row_cap = (2 * row_count + owner_count - 1) // owner_count
    coarse_rows = row_count // AGG
    total = coarse_rows * KC
    a_local, p_local = a_tiles[0, 0], p_tiles[0, 0]
    near, group = neighbours[0, 0], groups[0, 0]
    slot_local, aggregate = slots[0, 0], aggregates[0, 0]

    owners = aggregate // coarse_rows
    local_row = aggregate % coarse_rows
    indices = jnp.arange(row_count, dtype=jnp.int32)
    same_owner = owners[:, None] == owners[None, :]
    earlier = indices[:, None] > indices[None, :]
    rank = jnp.sum((same_owner & earlier).astype(jnp.int32), axis=1)
    chunks = min(CHUNKS, row_cap)
    width = row_cap // chunks
    position = (rank // width * owner_count + owners) * width + rank % width
    slot_total = owner_count * row_cap
    selector = jnp.arange(slot_total, dtype=jnp.int32)[:, None] == position[None, :]
    segments = local_row[:, None] * KC + slot_local
    meta = jnp.concatenate([jnp.ones_like(local_row)[:, None], segments], axis=1)
    meta_sent = jnp.sum(jnp.where(selector[:, :, None], meta[None], 0), axis=1)
    meta_sent = meta_sent.reshape(chunks, owner_count, width, touched + 1)
    meta_recv = lax.all_to_all(meta_sent, "gy", split_axis=1, concat_axis=1, tiled=True)
    meta_recv = meta_recv.reshape(chunks, owner_count * width, touched + 1)

    pieces = halo(p_local)
    coarse = None
    sent = []
    for chunk in range(chunks):
        steps = min(row_count, owner_count * width, row_count)
        active = rank // width == chunk
        count = jnp.sum(active.astype(jnp.int32))
        ahead = jnp.sum((active[None, :] & earlier).astype(jnp.int32), axis=1)
        wanted = jnp.minimum(jnp.arange(steps, dtype=jnp.int32), count - 1)
        chosen = active[None, :] & (ahead[None, :] == wanted[:, None])
        order = jnp.sum(jnp.where(chosen, indices[None, :], 0), axis=1)
        place = jnp.sum(jnp.where(chosen, (owners * width + rank % width)[None, :], 0), axis=1)
        sent.append(
            row_products(
                a_local, pieces, near, group, order, place, count[None],
                owner_count * width, touched,
            )
        )
    recv = [lax.all_to_all(s, "gy", split_axis=0, concat_axis=0, tiled=True) for s in sent]
    for chunk in range(chunks):
        coarse = coarse_sums(
            recv[chunk], meta_recv[chunk, :, 1:], meta_recv[chunk, :, 0], total, coarse
        )
    return coarse.reshape(1, 1, coarse_rows, KC, size, size)


def solution(mesh):
    return jax.shard_map(
        shards,
        mesh=mesh,
        in_specs=(
            P("gx", "gy", None, None, None, None),
            P("gx", "gy", None, None, None),
            P("gx", "gy", None, None),
            P("gx", "gy", None, None),
            P("gx", "gy", None, None),
            P("gx", "gy", None),
        ),
        out_specs=P("gx", "gy", None, None, None, None),
        check_vma=False,
    )
```

```python
import functools
import math

import jax
import jax.numpy as jnp
from jax import lax
from jax.experimental import pallas as pl
from jax.experimental.pallas import tpu as pltpu
from jax.sharding import PartitionSpec as P

KC = 27
AGG = 4
MESH = pl.DeviceIdType.MESH


def shifted(block, axis, step):
    count = lax.axis_size(axis)
    pairs = [(i, i + step) for i in range(count) if 0 <= i + step < count]
    return lax.ppermute(block, axis, pairs)


def halo(block):
    below, above = shifted(block, "gy", 1), shifted(block, "gy", -1)
    line = (below, block, above)
    low = [shifted(piece, "gx", 1) for piece in line]
    high = [shifted(piece, "gx", -1) for piece in line]
    return (*low, *line, *high)


def row_kernel(order, place, count, near, group, a_ref, *rest):
    pieces, (out_ref, table, sums, sems) = rest[:9], rest[9:]
    step = pl.program_id(0)
    tiles, rows = a_ref.shape[1], pieces[0].shape[0]
    touched = sums.shape[0]

    @pl.when(step == 0)
    def _():
        copies = [
            pltpu.make_async_copy(piece, table.at[pl.ds(j * rows, rows)], sems.at[j])
            for j, piece in enumerate(pieces)
        ]
        for copy in copies:
            copy.start()
        for copy in copies:
            copy.wait()

    @pl.when(step < count[0])
    def _():
        row = order[step]
        sums[...] = jnp.zeros_like(sums)
        for k in range(tiles):
            product = jnp.dot(
                a_ref[0, k], table[near[row, k]], preferred_element_type=jnp.float32
            )
            sums[group[row, k]] += product
        own = table[4 * rows + row]
        for f in range(touched):
            out_ref[0, f] = lax.dot_general(
                own,
                sums[f].astype(jnp.bfloat16),
                (((0,), (0,)), ((), ())),
                preferred_element_type=jnp.float32,
            ).astype(jnp.bfloat16)


def row_products(a_local, pieces, near, group, order, place, count, slot_total, touched):
    rows, tiles, size, _ = a_local.shape
    steps = order.shape[0]
    flops = 2 * steps * (tiles + touched) * size**3
    return pl.pallas_call(
        row_kernel,
        out_shape=jax.ShapeDtypeStruct((slot_total, touched, size, size), jnp.bfloat16),
        grid_spec=pltpu.PrefetchScalarGridSpec(
            num_scalar_prefetch=5,
            grid=(steps,),
            in_specs=[
                pl.BlockSpec(
                    (1, tiles, size, size), lambda i, order, *_: (order[i], 0, 0, 0)
                )
            ]
            + [pl.BlockSpec(memory_space=pl.ANY)] * 9,
            out_specs=pl.BlockSpec(
                (1, touched, size, size), lambda i, order, place, *_: (place[i], 0, 0, 0)
            ),
            scratch_shapes=[
                pltpu.VMEM((9 * rows, size, size), jnp.bfloat16),
                pltpu.VMEM((touched, size, size), jnp.float32),
                pltpu.SemaphoreType.DMA((9,)),
            ],
        ),
        compiler_params=pltpu.CompilerParams(vmem_limit_bytes=60 << 20),
        cost_estimate=pl.CostEstimate(
            flops=flops, bytes_accessed=2 * steps * (tiles + touched) * size**2, transcendentals=0
        ),
    )(order, place, count, near, group, a_local, *pieces)


def sum_kernel(segment, valid, recv_ref, out_ref):
    step = pl.program_id(0)

    @pl.when(step == 0)
    def _():
        out_ref[...] = jnp.zeros_like(out_ref)

    batch = recv_ref.shape[0]
    for j in range(batch):
        slot = step * batch + j

        @pl.when(valid[slot] > 0)
        def _():
            for f in range(recv_ref.shape[1]):
                out_ref[segment[slot, f]] += recv_ref[j, f].astype(jnp.float32)


def coarse_sums(recv, segment, valid, total):
    slot_total, touched, size, _ = recv.shape
    batch = math.gcd(slot_total, 4)
    return pl.pallas_call(
        sum_kernel,
        out_shape=jax.ShapeDtypeStruct((total, size, size), jnp.float32),
        grid_spec=pltpu.PrefetchScalarGridSpec(
            num_scalar_prefetch=2,
            grid=(slot_total // batch,),
            in_specs=[pl.BlockSpec((batch, touched, size, size), lambda i, *_: (i, 0, 0, 0))],
            out_specs=pl.BlockSpec((total, size, size), lambda i, *_: (0, 0, 0)),
        ),
        compiler_params=pltpu.CompilerParams(vmem_limit_bytes=60 << 20),
        cost_estimate=pl.CostEstimate(
            flops=slot_total * touched * size**2,
            bytes_accessed=(2 * slot_total * touched + 4 * total) * size**2,
            transcendentals=0,
        ),
    )(segment, valid, recv)


def partner(me, bits, count):
    if count & (count - 1):
        return (me + bits) % count
    target, unit = 0, 1
    while unit < count:
        bit = me // unit % 2
        target = target + unit * (1 - bit if bits & unit else bit)
        unit *= 2
    return target


def swap_kernel(count, width, sent, meta, recv, meta_recv, send_sems, recv_sems, local_sems):
    me = lax.axis_index("gy")
    block = lambda owner: pl.ds(owner * width, width)
    barrier = pltpu.get_barrier_semaphore()
    for bits in range(1, count):
        pl.semaphore_signal(
            barrier, inc=1, device_id={"gy": partner(me, bits, count)}, device_id_type=MESH
        )
    pl.semaphore_wait(barrier, count - 1)
    copies = []
    for bits in range(1, count):
        target = partner(me, bits, count)
        for j, (source, place) in enumerate(
            ((meta.at[target], meta_recv.at[me]), (sent.at[block(target)], recv.at[block(me)]))
        ):
            copies.append(
                pltpu.make_async_remote_copy(
                    src_ref=source,
                    dst_ref=place,
                    send_sem=send_sems.at[j, bits - 1],
                    recv_sem=recv_sems.at[j, bits - 1],
                    device_id={"gy": target},
                    device_id_type=MESH,
                )
            )
    copies.append(pltpu.make_async_copy(meta.at[me], meta_recv.at[me], local_sems.at[0]))
    copies.append(
        pltpu.make_async_copy(sent.at[block(me)], recv.at[block(me)], local_sems.at[1])
    )
    for copy in copies:
        copy.start()
    for copy in copies:
        copy.wait()


def swapped(sent, meta, count, width):
    return pl.pallas_call(
        functools.partial(swap_kernel, count, width),
        out_shape=(
            jax.ShapeDtypeStruct(sent.shape, sent.dtype),
            jax.ShapeDtypeStruct(meta.shape, meta.dtype),
        ),
        in_specs=[pl.BlockSpec(memory_space=pl.ANY)] * 2,
        out_specs=[pl.BlockSpec(memory_space=pl.ANY)] * 2,
        scratch_shapes=[
            pltpu.SemaphoreType.DMA((2, count - 1)),
            pltpu.SemaphoreType.DMA((2, count - 1)),
            pltpu.SemaphoreType.DMA((2,)),
        ],
        compiler_params=pltpu.CompilerParams(
            collective_id=0, has_side_effects=True, vmem_limit_bytes=60 << 20
        ),
    )(sent, meta)


def shards(a_tiles, p_tiles, neighbours, groups, slots, aggregates):
    row_count = a_tiles.shape[2]
    touched = slots.shape[-1]
    size = a_tiles.shape[-1]
    owner_count = lax.axis_size("gy")
    row_cap = (2 * row_count + owner_count - 1) // owner_count
    coarse_rows = row_count // AGG
    total = coarse_rows * KC
    a_local, p_local = a_tiles[0, 0], p_tiles[0, 0]
    near, group = neighbours[0, 0], groups[0, 0]
    slot_local, aggregate = slots[0, 0], aggregates[0, 0]

    owners = aggregate // coarse_rows
    local_row = aggregate % coarse_rows
    indices = jnp.arange(row_count, dtype=jnp.int32)
    same_owner = owners[:, None] == owners[None, :]
    earlier = indices[:, None] > indices[None, :]
    rank = jnp.sum((same_owner & earlier).astype(jnp.int32), axis=1)
    position = owners * row_cap + rank
    slot_total = owner_count * row_cap
    selector = jnp.arange(slot_total, dtype=jnp.int32)[:, None] == position[None, :]
    segments = local_row[:, None] * KC + slot_local
    meta = jnp.concatenate([jnp.ones_like(local_row)[:, None], segments], axis=1)
    meta_sent = jnp.sum(jnp.where(selector[:, :, None], meta[None], 0), axis=1)
    meta_sent = meta_sent.reshape(owner_count, row_cap, touched + 1)
    meta_sent = jnp.pad(meta_sent, ((0, 0), (0, -row_cap % 8), (0, -(touched + 1) % 128)))

    sent = row_products(
        a_local, halo(p_local), near, group, indices, position,
        jnp.full((1,), row_count, jnp.int32), slot_total, touched,
    )
    recv, meta_recv = swapped(sent, meta_sent, owner_count, row_cap)
    meta_recv = meta_recv[:, :row_cap, : touched + 1].reshape(slot_total, touched + 1)
    coarse = coarse_sums(recv, meta_recv[:, 1:], meta_recv[:, 0], total)
    return coarse.reshape(1, 1, coarse_rows, KC, size, size)


def solution(mesh):
    return jax.shard_map(
        shards,
        mesh=mesh,
        in_specs=(
            P("gx", "gy", None, None, None, None),
            P("gx", "gy", None, None, None),
            P("gx", "gy", None, None),
            P("gx", "gy", None, None),
            P("gx", "gy", None, None),
            P("gx", "gy", None),
        ),
        out_specs=P("gx", "gy", None, None, None, None),
        check_vma=False,
    )
```

```python
import functools

import jax
import jax.numpy as jnp
from jax import lax
from jax.experimental import pallas as pl
from jax.experimental.pallas import tpu as pltpu
from jax.sharding import PartitionSpec as P

KC = 27
AGG = 4
MESH = pl.DeviceIdType.MESH


def shifted(block, axis, step):
    count = lax.axis_size(axis)
    pairs = [(i, i + step) for i in range(count) if 0 <= i + step < count]
    return lax.ppermute(block, axis, pairs)


def halo(block):
    below, above = shifted(block, "gy", 1), shifted(block, "gy", -1)
    line = (below, block, above)
    low = [shifted(piece, "gx", 1) for piece in line]
    high = [shifted(piece, "gx", -1) for piece in line]
    return (*low, *line, *high)


def row_kernel(order, place, count, near, group, a_hbm, *rest):
    pieces, (out_ref, a_ref, table, sums, sems, row_sems) = rest[:9], rest[9:]
    step = pl.program_id(0)
    tiles, rows = a_ref.shape[1], pieces[0].shape[0]
    touched = sums.shape[0]

    @pl.when(step == 0)
    def _():
        copies = [
            pltpu.make_async_copy(piece, table.at[pl.ds(j * rows, rows)], sems.at[j])
            for j, piece in enumerate(pieces)
        ]
        for copy in copies:
            copy.start()
        for j in range(rows):
            pltpu.make_async_copy(a_hbm.at[j], a_ref.at[j], row_sems.at[j]).start()
        for copy in copies:
            copy.wait()

    pltpu.make_async_copy(a_hbm.at[step], a_ref.at[step], row_sems.at[step]).wait()

    @pl.when(step < count[0])
    def _():
        row = order[step]
        sums[...] = jnp.zeros_like(sums)
        for k in range(tiles):
            product = jnp.dot(
                a_ref[row, k], table[near[row, k]], preferred_element_type=jnp.float32
            )
            sums[group[row, k]] += product
        own = table[4 * rows + row]
        for f in range(touched):
            out_ref[0, f] = lax.dot_general(
                own,
                sums[f].astype(jnp.bfloat16),
                (((0,), (0,)), ((), ())),
                preferred_element_type=jnp.float32,
            ).astype(jnp.bfloat16)


def row_products(a_local, pieces, near, group, order, place, count, slot_total, touched):
    rows, tiles, size, _ = a_local.shape
    steps = order.shape[0]
    flops = 2 * steps * (tiles + touched) * size**3
    return pl.pallas_call(
        row_kernel,
        out_shape=jax.ShapeDtypeStruct((slot_total, touched, size, size), jnp.bfloat16),
        grid_spec=pltpu.PrefetchScalarGridSpec(
            num_scalar_prefetch=5,
            grid=(steps,),
            in_specs=[pl.BlockSpec(memory_space=pl.ANY)] * 10,
            out_specs=pl.BlockSpec(
                (1, touched, size, size), lambda i, order, place, *_: (place[i], 0, 0, 0)
            ),
            scratch_shapes=[
                pltpu.VMEM(a_local.shape, jnp.bfloat16),
                pltpu.VMEM((9 * rows, size, size), jnp.bfloat16),
                pltpu.VMEM((touched, size, size), jnp.float32),
                pltpu.SemaphoreType.DMA((9,)),
                pltpu.SemaphoreType.DMA((rows,)),
            ],
        ),
        compiler_params=pltpu.CompilerParams(vmem_limit_bytes=60 << 20),
        cost_estimate=pl.CostEstimate(
            flops=flops, bytes_accessed=2 * steps * (tiles + touched) * size**2, transcendentals=0
        ),
    )(order, place, count, near, group, a_local, *pieces)


def sum_kernel(segment, valid, recv_hbm, out_ref, recv_ref, sems):
    step = pl.program_id(0)

    @pl.when(step == 0)
    def _():
        for j in range(recv_ref.shape[0]):
            pltpu.make_async_copy(recv_hbm.at[j], recv_ref.at[j], sems.at[j]).start()
        out_ref[...] = jnp.zeros_like(out_ref)

    pltpu.make_async_copy(recv_hbm.at[step], recv_ref.at[step], sems.at[step]).wait()

    @pl.when(valid[step] > 0)
    def _():
        for f in range(recv_ref.shape[1]):
            out_ref[segment[step, f]] += recv_ref[step, f].astype(jnp.float32)


def coarse_sums(recv, segment, valid, total):
    slot_total, touched, size, _ = recv.shape
    return pl.pallas_call(
        sum_kernel,
        out_shape=jax.ShapeDtypeStruct((total, size, size), jnp.float32),
        grid_spec=pltpu.PrefetchScalarGridSpec(
            num_scalar_prefetch=2,
            grid=(slot_total,),
            in_specs=[pl.BlockSpec(memory_space=pl.ANY)],
            out_specs=pl.BlockSpec((total, size, size), lambda i, *_: (0, 0, 0)),
            scratch_shapes=[
                pltpu.VMEM(recv.shape, recv.dtype),
                pltpu.SemaphoreType.DMA((slot_total,)),
            ],
        ),
        compiler_params=pltpu.CompilerParams(vmem_limit_bytes=60 << 20),
        cost_estimate=pl.CostEstimate(
            flops=slot_total * touched * size**2,
            bytes_accessed=(2 * slot_total * touched + 4 * total) * size**2,
            transcendentals=0,
        ),
    )(segment, valid, recv)


def partner(me, bits, count):
    if count & (count - 1):
        return (me + bits) % count
    target, unit = 0, 1
    while unit < count:
        bit = me // unit % 2
        target = target + unit * (1 - bit if bits & unit else bit)
        unit *= 2
    return target


def swap_kernel(count, width, sent, meta, recv, meta_recv, send_sems, recv_sems, local_sems):
    me = lax.axis_index("gy")
    block = lambda owner: pl.ds(owner * width, width)
    barrier = pltpu.get_barrier_semaphore()
    for bits in range(1, count):
        pl.semaphore_signal(
            barrier, inc=1, device_id={"gy": partner(me, bits, count)}, device_id_type=MESH
        )
    pl.semaphore_wait(barrier, count - 1)
    copies = []
    for bits in range(1, count):
        target = partner(me, bits, count)
        for j, (source, place) in enumerate(
            ((meta.at[target], meta_recv.at[me]), (sent.at[block(target)], recv.at[block(me)]))
        ):
            copies.append(
                pltpu.make_async_remote_copy(
                    src_ref=source,
                    dst_ref=place,
                    send_sem=send_sems.at[j, bits - 1],
                    recv_sem=recv_sems.at[j, bits - 1],
                    device_id={"gy": target},
                    device_id_type=MESH,
                )
            )
    copies.append(pltpu.make_async_copy(meta.at[me], meta_recv.at[me], local_sems.at[0]))
    copies.append(
        pltpu.make_async_copy(sent.at[block(me)], recv.at[block(me)], local_sems.at[1])
    )
    for copy in copies:
        copy.start()
    for copy in copies:
        copy.wait()


def swapped(sent, meta, count, width):
    return pl.pallas_call(
        functools.partial(swap_kernel, count, width),
        out_shape=(
            jax.ShapeDtypeStruct(sent.shape, sent.dtype),
            jax.ShapeDtypeStruct(meta.shape, meta.dtype),
        ),
        in_specs=[pl.BlockSpec(memory_space=pl.ANY)] * 2,
        out_specs=[pl.BlockSpec(memory_space=pl.ANY)] * 2,
        scratch_shapes=[
            pltpu.SemaphoreType.DMA((2, count - 1)),
            pltpu.SemaphoreType.DMA((2, count - 1)),
            pltpu.SemaphoreType.DMA((2,)),
        ],
        compiler_params=pltpu.CompilerParams(
            collective_id=0, has_side_effects=True, vmem_limit_bytes=60 << 20
        ),
    )(sent, meta)


def shards(a_tiles, p_tiles, neighbours, groups, slots, aggregates):
    row_count = a_tiles.shape[2]
    touched = slots.shape[-1]
    size = a_tiles.shape[-1]
    owner_count = lax.axis_size("gy")
    row_cap = (2 * row_count + owner_count - 1) // owner_count
    coarse_rows = row_count // AGG
    total = coarse_rows * KC
    a_local, p_local = a_tiles[0, 0], p_tiles[0, 0]
    near, group = neighbours[0, 0], groups[0, 0]
    slot_local, aggregate = slots[0, 0], aggregates[0, 0]

    owners = aggregate // coarse_rows
    local_row = aggregate % coarse_rows
    indices = jnp.arange(row_count, dtype=jnp.int32)
    same_owner = owners[:, None] == owners[None, :]
    earlier = indices[:, None] > indices[None, :]
    rank = jnp.sum((same_owner & earlier).astype(jnp.int32), axis=1)
    position = owners * row_cap + rank
    slot_total = owner_count * row_cap
    selector = jnp.arange(slot_total, dtype=jnp.int32)[:, None] == position[None, :]
    segments = local_row[:, None] * KC + slot_local
    meta = jnp.concatenate([jnp.ones_like(local_row)[:, None], segments], axis=1)
    meta_sent = jnp.sum(jnp.where(selector[:, :, None], meta[None], 0), axis=1)
    meta_sent = meta_sent.reshape(owner_count, row_cap, touched + 1)
    meta_sent = jnp.pad(meta_sent, ((0, 0), (0, -row_cap % 8), (0, -(touched + 1) % 128)))

    sent = row_products(
        a_local, halo(p_local), near, group, indices, position,
        jnp.full((1,), row_count, jnp.int32), slot_total, touched,
    )
    recv, meta_recv = swapped(sent, meta_sent, owner_count, row_cap)
    meta_recv = meta_recv[:, :row_cap, : touched + 1].reshape(slot_total, touched + 1)
    coarse = coarse_sums(recv, meta_recv[:, 1:], meta_recv[:, 0], total)
    return coarse.reshape(1, 1, coarse_rows, KC, size, size)


def solution(mesh):
    return jax.shard_map(
        shards,
        mesh=mesh,
        in_specs=(
            P("gx", "gy", None, None, None, None),
            P("gx", "gy", None, None, None),
            P("gx", "gy", None, None),
            P("gx", "gy", None, None),
            P("gx", "gy", None, None),
            P("gx", "gy", None),
        ),
        out_specs=P("gx", "gy", None, None, None, None),
        check_vma=False,
    )
```
